32 devices in a mesh: dp: 8 (over y, x, core), tensor: 4 (over z).
Axes of the slice: x: 2, y: 2, z: 4, core: 2. Of those that a mesh axis runs over, the one named last changes fastest.
Arguments:
- tokens: bfloat16 [5120, 1024], P(('dp', 'tensor')), may hold values from -6 to 6
- cotangent: float32 [5120, 1024], P(('dp', 'tensor')), may hold values from -6 to 6
- image_group: int32 [7], replicated, may hold values from 0 to 7, as said below
- first_norm_gain_param: float32 [1024], P(('dp', 'tensor')), may hold values from 0.1 to 1.9
- first_norm_bias: float32 [1024], P(('dp', 'tensor')), may hold values from -3 to 3
- w_qkv: bfloat16 [1024, 3072], P('dp', 'tensor'), may hold values from -0.1875 to 0.1875
- qv_bias: float32 [2048], P(('dp', 'tensor')), may hold values from -3 to 3
- w_out: bfloat16 [1024, 1024], P('tensor', 'dp'), may hold values from -1 to 1
- out_bias: float32 [1024], P(('dp', 'tensor')), may hold values from -3 to 3
- second_norm_gain_param: float32 [1024], P(('dp', 'tensor')), may hold values from 0.1 to 1.9
- second_norm_bias: float32 [1024], P(('dp', 'tensor')), may hold values from -3 to 3
- w_up: bfloat16 [1024, 4096], P('dp', 'tensor'), may hold values from -0.1875 to 0.1875
- up_bias: float32 [4096], P(('dp', 'tensor')), may hold values from -3 to 3
- w_down: bfloat16 [4096, 1024], P('tensor', 'dp'), may hold values from -0.09375 to 0.09375
- down_bias: float32 [1024], P(('dp', 'tensor')), may hold values from -3 to 3
Outputs:
- output: bfloat16 [5120, 1024], P(('dp', 'tensor'))
- layer_input_gradient: float32 [5120, 1024], P(('dp', 'tensor'))
- ln1_gain_grad: float32 [1024], P(('dp', 'tensor'))
- ln1_bias_grad: float32 [1024], P(('dp', 'tensor'))
- w_qkv_grad: float32 [1024, 3072], P('dp', 'tensor')
- qv_bias_grad: float32 [2048], P(('dp', 'tensor'))
- w_out_grad: float32 [1024, 1024], P('tensor', 'dp')
- out_bias_grad: float32 [1024], P(('dp', 'tensor'))
- ln2_gain_grad: float32 [1024], P(('dp', 'tensor'))
- ln2_bias_grad: float32 [1024], P(('dp', 'tensor'))
- w_up_grad: float32 [1024, 4096], P('dp', 'tensor')
- up_bias_grad: float32 [4096], P(('dp', 'tensor'))
- w_down_grad: float32 [4096, 1024], P('tensor', 'dp')
- down_bias_grad: float32 [1024], P(('dp', 'tensor'))
The draws below stay inside these ranges and needn't reach their ends.
Inputs may be any that keep to these rules, and one draw needn't show every extreme that they name: Group image_group[i] holds image i; 1 group hold 0 images and all others 1.
All inputs are finite; a program needn't handle non-finite values.
Results may differ from the reference program's by a relative error of at most 0.015.
Values may be sent and summed in bfloat16 or wider, within the bound.
A program may use at most 128 MiB of HBM per device.

```python
import jax
import jax.numpy as jnp
from jax import lax

D = 1024
HEADS = 16
HEAD_DIM = 64
FF = 4096
SEQ = 577
SEQ_PAD = 640
SLOTS = 1
IMAGES = 7
TOKENS = 5120
N_DP = 8
N_TENSOR = 4


def draw_image_group(key, part):
    order = jax.random.permutation(key, N_DP)
    index = jnp.arange(IMAGES, dtype=jnp.int32) % N_DP
    return order[index].astype(jnp.int32)


def shard_levels(rng, shape, cuts, low, largest):
    factor_of = 1.0
    for axis_at, shards_of in cuts:
        steps = jax.random.uniform(jax.random.fold_in(jax.random.fold_in(rng, 6), axis_at), (shards_of,), jnp.float32, low / len(cuts), largest / len(cuts))
        factor_of = factor_of * jnp.repeat(jnp.exp(steps), shape[axis_at] // shards_of).reshape((-1,) + (1,) * (len(shape) - 1 - axis_at))
    return factor_of


def normal_values(rng, dims, scale, most, split=(), held_as=jnp.bfloat16):
    level = shard_levels(rng, dims, split, -0.22, 0.18) if split else 1.0
    entries = jax.random.normal(rng, dims, jnp.float32) * scale * level
    return jnp.minimum(jnp.maximum(entries, -most), most).astype(held_as)


def setup_inputs(seed: int = 0) -> dict:
    key_list = jax.random.split(jax.random.key(seed), 16)
    tokens = normal_values(key_list[0], (TOKENS, D), 1.0, 6.0, ((0, 32),))
    cotangent = normal_values(key_list[1], (TOKENS, D), 1.0, 6.0, ((0, 32),), jnp.float32)
    image_group = draw_image_group(jax.random.fold_in(key_list[15], 71), 0)
    first_norm_gain_param = jnp.clip(1.0 + 0.18 * jax.random.normal(key_list[3], (D,), jnp.float32), 0.1, 1.9)
    first_norm_bias = normal_values(key_list[4], (D,), 0.5, 3.0, ((0, 32),), jnp.float32)
    w_qkv = normal_values(key_list[5], (D, 3 * D), D ** -0.5, 0.1875, ((0, 8), (1, 4)))
    qv_bias = normal_values(key_list[6], (2 * D,), 0.5, 3.0, ((0, 32),), jnp.float32)
    w_out = normal_values(key_list[7], (D, D), (D // 24) ** -0.5, 1.0, ((0, 4), (1, 8)))
    out_bias = normal_values(key_list[8], (D,), 0.5, 3.0, ((0, 32),), jnp.float32)
    second_norm_gain_param = jnp.clip(1.0 + 0.18 * jax.random.normal(key_list[9], (D,), jnp.float32), 0.1, 1.9)
    second_norm_bias = normal_values(key_list[10], (D,), 0.5, 3.0, ((0, 32),), jnp.float32)
    w_up = normal_values(key_list[11], (D, FF), D ** -0.5, 0.1875, ((0, 8), (1, 4)))
    up_bias = normal_values(key_list[12], (FF,), 0.5, 3.0, ((0, 32),), jnp.float32)
    w_down = normal_values(key_list[13], (FF, D), FF ** -0.5, 0.09375, ((0, 4), (1, 8)))
    down_bias = normal_values(key_list[14], (D,), 0.5, 3.0, ((0, 32),), jnp.float32)
    return dict(tokens=tokens, cotangent=cotangent, image_group=image_group, first_norm_gain_param=first_norm_gain_param, first_norm_bias=first_norm_bias, w_qkv=w_qkv, qv_bias=qv_bias, w_out=w_out, out_bias=out_bias, second_norm_gain_param=second_norm_gain_param, second_norm_bias=second_norm_bias, w_up=w_up, up_bias=up_bias, w_down=w_down, down_bias=down_bias)


EPS = 1e-06
NEG_LARGE = -1e+30
ROOT_HALF = 0.7071067811865476
INV_ROOT_TAU = 0.3989422804014327

def apply_layer_norm(values, norm_gain_vector, norm_shift_vector):
    average = lax.optimization_barrier(jnp.mean(values, axis=1, keepdims=True))
    mean_removed = values - average
    variance = lax.optimization_barrier(jnp.mean(mean_removed * mean_removed, axis=1, keepdims=True))
    inverse_deviation = lax.rsqrt(variance + EPS)
    standardized_rows = mean_removed * inverse_deviation
    return (standardized_rows * norm_gain_vector + norm_shift_vector, standardized_rows, inverse_deviation)

def layer_norm_backward(incoming_gradient, standardized_rows, inverse_deviation, norm_gain_vector):
    gain_scaled_gradient = incoming_gradient * norm_gain_vector
    return inverse_deviation * (gain_scaled_gradient - lax.optimization_barrier(jnp.mean(gain_scaled_gradient, axis=1, keepdims=True)) - standardized_rows * lax.optimization_barrier(jnp.mean(gain_scaled_gradient * standardized_rows, axis=1, keepdims=True)))

def gelu_value(hidden):
    return 0.5 * hidden * (1.0 + jax.scipy.special.erf(hidden * ROOT_HALF))

def gelu_slope(hidden):
    return 0.5 * (1.0 + jax.scipy.special.erf(hidden * ROOT_HALF)) + hidden * INV_ROOT_TAU * jnp.exp(-0.5 * hidden * hidden)

def masked_scores(queries, keys, key_valid):
    scores = jnp.einsum('qhd,khd->hqk', queries.astype(jnp.float32), keys.astype(jnp.float32)) * HEAD_DIM ** (-0.5)
    return jnp.where(key_valid[None, None, :], scores, NEG_LARGE)

def attend_slot(items):
    queries, keys, values, key_valid = items
    scores = masked_scores(queries, keys, key_valid)
    top = lax.optimization_barrier(jnp.max(scores, axis=2, keepdims=True))
    total = lax.optimization_barrier(jnp.sum(jnp.exp(scores - top), axis=2, keepdims=True))
    logsum = top + jnp.log(total)
    probs = jnp.exp(scores - logsum).astype(jnp.bfloat16)
    mixed = jnp.einsum('hqk,khd->qhd', probs.astype(jnp.float32), values.astype(jnp.float32)).astype(jnp.bfloat16)
    return (mixed, logsum[:, :, 0])

def attend_back(items):
    queries, keys, values, key_valid, logsum, mixed, grad_mixed = items
    scores = masked_scores(queries, keys, key_valid)
    probs = jnp.exp(scores - logsum[:, :, None])
    rounded = probs.astype(jnp.bfloat16).astype(jnp.float32)
    grad_wide = grad_mixed.astype(jnp.float32)
    grad_values = jnp.einsum('hqk,qhd->khd', rounded, grad_wide)
    grad_probs = jnp.einsum('qhd,khd->hqk', grad_wide, values.astype(jnp.float32))
    delta = lax.optimization_barrier(jnp.sum(grad_wide * mixed.astype(jnp.float32), axis=2)).T
    grad_scores = (probs * (grad_probs - delta[:, :, None]) * HEAD_DIM ** (-0.5)).astype(jnp.bfloat16).astype(jnp.float32)
    grad_queries = jnp.einsum('hqk,khd->qhd', grad_scores, keys.astype(jnp.float32))
    grad_keys = jnp.einsum('hqk,qhd->khd', grad_scores, queries.astype(jnp.float32))
    return (grad_queries, grad_keys, grad_values)

def reference(tokens, cotangent, image_group, first_norm_gain_param, first_norm_bias, w_qkv, qv_bias, w_out, out_bias, second_norm_gain_param, second_norm_bias, w_up, up_bias, w_down, down_bias):
    group_rows = SLOTS * SEQ_PAD
    heads_part = HEADS // N_TENSOR
    counts = lax.optimization_barrier(jnp.sum((image_group[None, :] == jnp.arange(N_DP, dtype=jnp.int32)[:, None]).astype(jnp.int32), axis=1))
    bias_grid = qv_bias.reshape(N_TENSOR, 2, heads_part, HEAD_DIM)
    query_shift = bias_grid[:, 0].reshape(HEADS, HEAD_DIM)
    value_shift = bias_grid[:, 1].reshape(HEADS, HEAD_DIM)
    positions = jnp.arange(group_rows, dtype=jnp.int32)

    def one_group(carry, items):
        block_in, block_cot, occupied = items
        valid = (positions % SEQ_PAD < SEQ) & (positions // SEQ_PAD < occupied)
        row_valid = valid.astype(jnp.float32)[:, None]
        key_valid = valid.reshape(SLOTS, SEQ_PAD)
        layer_inputs = block_in.astype(jnp.float32)
        first_normed_rows, first_standardized, first_inverse_deviation = apply_layer_norm(layer_inputs, first_norm_gain_param, first_norm_bias)
        first_normed_rows = first_normed_rows.astype(jnp.bfloat16)
        projected = jnp.dot(first_normed_rows, w_qkv, preferred_element_type=jnp.float32).reshape(group_rows, N_TENSOR, 3, heads_part, HEAD_DIM)
        queries = (projected[:, :, 0].reshape(group_rows, HEADS, HEAD_DIM) + query_shift).astype(jnp.bfloat16)
        keys = projected[:, :, 1].reshape(group_rows, HEADS, HEAD_DIM).astype(jnp.bfloat16)
        values = (projected[:, :, 2].reshape(group_rows, HEADS, HEAD_DIM) + value_shift).astype(jnp.bfloat16)
        shaped = (queries.reshape(SLOTS, SEQ_PAD, HEADS, HEAD_DIM), keys.reshape(SLOTS, SEQ_PAD, HEADS, HEAD_DIM), values.reshape(SLOTS, SEQ_PAD, HEADS, HEAD_DIM), key_valid)
        mixed, logsum = lax.map(attend_slot, shaped)
        mixed_rows = mixed.reshape(group_rows, D)
        residual_stream = layer_inputs + jnp.dot(mixed_rows, w_out, preferred_element_type=jnp.float32) + out_bias
        second_normed_rows, second_standardized, second_inverse_deviation = apply_layer_norm(residual_stream, second_norm_gain_param, second_norm_bias)
        second_normed_rows = second_normed_rows.astype(jnp.bfloat16)
        hidden = jnp.dot(second_normed_rows, w_up, preferred_element_type=jnp.float32) + up_bias
        activated = gelu_value(hidden).astype(jnp.bfloat16)
        output = (row_valid * (residual_stream + jnp.dot(activated, w_down, preferred_element_type=jnp.float32) + down_bias)).astype(jnp.bfloat16)
        output_gradient = row_valid * block_cot
        grad_out_b = output_gradient.astype(jnp.bfloat16)
        down_projection_gradient = jnp.dot(activated.T, grad_out_b, preferred_element_type=jnp.float32)
        hidden_gradient = jnp.dot(grad_out_b, w_down.T, preferred_element_type=jnp.float32) * gelu_slope(hidden)
        grad_hidden_b = hidden_gradient.astype(jnp.bfloat16)
        up_projection_gradient = jnp.dot(second_normed_rows.T, grad_hidden_b, preferred_element_type=jnp.float32)
        second_normed_gradient = jnp.dot(grad_hidden_b, w_up.T, preferred_element_type=jnp.float32)
        residual_gradient = output_gradient + layer_norm_backward(second_normed_gradient, second_standardized, second_inverse_deviation, second_norm_gain_param)
        grad_resid_b = residual_gradient.astype(jnp.bfloat16)
        output_projection_gradient = jnp.dot(mixed_rows.T, grad_resid_b, preferred_element_type=jnp.float32)
        grad_mixed = jnp.dot(grad_resid_b, w_out.T, preferred_element_type=jnp.float32).astype(jnp.bfloat16)
        back_items = shaped + (logsum, mixed, grad_mixed.reshape(SLOTS, SEQ_PAD, HEADS, HEAD_DIM))
        grad_queries, grad_keys, grad_values = lax.map(attend_back, back_items)
        grad_queries = grad_queries.reshape(group_rows, HEADS, HEAD_DIM)
        grad_keys = grad_keys.reshape(group_rows, HEADS, HEAD_DIM)
        grad_values = grad_values.reshape(group_rows, HEADS, HEAD_DIM)
        query_value_bias_gradient = jnp.stack([lax.optimization_barrier(jnp.sum(grad_queries, axis=0)).reshape(N_TENSOR, heads_part, HEAD_DIM), lax.optimization_barrier(jnp.sum(grad_values, axis=0)).reshape(N_TENSOR, heads_part, HEAD_DIM)], axis=1).reshape(2 * D)
        grad_projected = jnp.stack([grad_queries.reshape(group_rows, N_TENSOR, heads_part, HEAD_DIM), grad_keys.reshape(group_rows, N_TENSOR, heads_part, HEAD_DIM), grad_values.reshape(group_rows, N_TENSOR, heads_part, HEAD_DIM)], axis=2).reshape(group_rows, 3 * D).astype(jnp.bfloat16)
        query_key_value_gradient = jnp.dot(first_normed_rows.T, grad_projected, preferred_element_type=jnp.float32)
        first_normed_gradient = jnp.dot(grad_projected, w_qkv.T, preferred_element_type=jnp.float32)
        layer_input_gradient = residual_gradient + layer_norm_backward(first_normed_gradient, first_standardized, first_inverse_deviation, first_norm_gain_param)
        gradient_terms = (lax.optimization_barrier(jnp.sum(first_normed_gradient * first_standardized, axis=0)), lax.optimization_barrier(jnp.sum(first_normed_gradient, axis=0)), query_key_value_gradient, query_value_bias_gradient, output_projection_gradient, lax.optimization_barrier(jnp.sum(residual_gradient, axis=0)), lax.optimization_barrier(jnp.sum(second_normed_gradient * second_standardized, axis=0)), lax.optimization_barrier(jnp.sum(second_normed_gradient, axis=0)), up_projection_gradient, lax.optimization_barrier(jnp.sum(hidden_gradient, axis=0)), down_projection_gradient, lax.optimization_barrier(jnp.sum(output_gradient, axis=0)))
        carry = tuple((total + term for total, term in zip(carry, gradient_terms)))
        return (carry, (output, layer_input_gradient))
    start = (jnp.zeros((D,), jnp.float32), jnp.zeros((D,), jnp.float32), jnp.zeros((D, 3 * D), jnp.float32), jnp.zeros((2 * D,), jnp.float32), jnp.zeros((D, D), jnp.float32), jnp.zeros((D,), jnp.float32), jnp.zeros((D,), jnp.float32), jnp.zeros((D,), jnp.float32), jnp.zeros((D, FF), jnp.float32), jnp.zeros((FF,), jnp.float32), jnp.zeros((FF, D), jnp.float32), jnp.zeros((D,), jnp.float32))
    sums, (outputs, input_grads) = lax.scan(one_group, start, (tokens.reshape(N_DP, group_rows, D), cotangent.reshape(N_DP, group_rows, D), counts))
    return (outputs.reshape(N_DP * group_rows, D), input_grads.reshape(N_DP * group_rows, D), sums[0], sums[1], sums[2], sums[3], sums[4], sums[5], sums[6], sums[7], sums[8], sums[9], sums[10], sums[11])
```

```python
import jax
import jax.numpy as jnp
from jax import lax
from jax.sharding import PartitionSpec as P

D = 1024
HEAD_DIM = 64
FF = 4096
SEQ = 577
SEQ_PAD = 640


EPS = 1e-06
NEG_LARGE = -1e30
ROOT_HALF = 0.7071067811865476
INV_ROOT_TAU = 0.3989422804014327


def apply_layer_norm(values, norm_gain_vector, norm_shift_vector):
    average = jnp.mean(values, axis=1, keepdims=True)
    mean_removed = values - average
    variance = jnp.mean(mean_removed * mean_removed, axis=1, keepdims=True)
    inverse_deviation = lax.rsqrt(variance + EPS)
    standardized_rows = mean_removed * inverse_deviation
    return (
        standardized_rows * norm_gain_vector + norm_shift_vector,
        standardized_rows,
        inverse_deviation,
    )


def layer_norm_backward(incoming_gradient, standardized_rows, inverse_deviation, norm_gain_vector):
    gain_scaled_gradient = incoming_gradient * norm_gain_vector
    return inverse_deviation * (
        gain_scaled_gradient
        - jnp.mean(gain_scaled_gradient, axis=1, keepdims=True)
        - standardized_rows
        * jnp.mean(gain_scaled_gradient * standardized_rows, axis=1, keepdims=True)
    )


def gelu_value(hidden):
    return 0.5 * hidden * (1.0 + jax.scipy.special.erf(hidden * ROOT_HALF))


def gelu_slope(hidden):
    return 0.5 * (
        1.0 + jax.scipy.special.erf(hidden * ROOT_HALF)
    ) + hidden * INV_ROOT_TAU * jnp.exp(-0.5 * hidden * hidden)


def left_product(first, second):
    return lax.dot_general(
        first, second, (((0,), (0,)), ((), ())), preferred_element_type=jnp.float32
    )


def right_product(first, second):
    return lax.dot_general(
        first, second, (((1,), (1,)), ((), ())), preferred_element_type=jnp.float32
    )


def gather_rows(values):
    return lax.all_gather(values, "tensor", axis=0, tiled=True)


def scatter_rows(values):
    return lax.psum_scatter(
        values.astype(jnp.bfloat16), "tensor", scatter_dimension=0, tiled=True
    ).astype(jnp.float32)


def gather_weights(w_qkv, w_out, w_up, w_down):
    return (
        lax.all_gather(w_qkv, "dp", axis=0, tiled=True),
        lax.all_gather(w_out, "dp", axis=1, tiled=True),
        lax.all_gather(w_up, "dp", axis=0, tiled=True),
        lax.all_gather(w_down, "dp", axis=1, tiled=True),
    )


def reduce_grads(row_split, column_split):
    return (
        lax.psum_scatter(
            row_split.astype(jnp.bfloat16), "dp", scatter_dimension=0, tiled=True
        ).astype(jnp.float32),
        lax.psum_scatter(
            column_split.astype(jnp.bfloat16), "dp", scatter_dimension=1, tiled=True
        ).astype(jnp.float32),
    )


def masked_scores(queries, keys, key_valid):
    scores = jnp.einsum(
        "qhd,khd->hqk", queries, keys, preferred_element_type=jnp.float32
    ) * HEAD_DIM ** (-0.5)
    return jnp.where(key_valid[None, None, :], scores, NEG_LARGE)


def attend_slot(items):
    queries, keys, values, key_valid = items
    scores = masked_scores(queries, keys, key_valid)
    top = jnp.max(scores, axis=2, keepdims=True)
    total = jnp.sum(jnp.exp(scores - top), axis=2, keepdims=True)
    logsum = top + jnp.log(total)
    probs = jnp.exp(scores - logsum).astype(jnp.bfloat16)
    mixed = jnp.einsum("hqk,khd->qhd", probs, values, preferred_element_type=jnp.float32).astype(
        jnp.bfloat16
    )
    return (mixed, logsum[:, :, 0])


def attend_back(items):
    queries, keys, values, key_valid, logsum, mixed, grad_mixed = items
    scores = masked_scores(queries, keys, key_valid)
    probs = jnp.exp(scores - logsum[:, :, None])
    rounded = probs.astype(jnp.bfloat16)
    grad_values = jnp.einsum(
        "hqk,qhd->khd", rounded, grad_mixed, preferred_element_type=jnp.float32
    )
    grad_probs = jnp.einsum("qhd,khd->hqk", grad_mixed, values, preferred_element_type=jnp.float32)
    delta = jnp.sum(grad_mixed.astype(jnp.float32) * mixed.astype(jnp.float32), axis=2).T
    grad_scores = (probs * (grad_probs - delta[:, :, None]) * HEAD_DIM ** (-0.5)).astype(
        jnp.bfloat16
    )
    grad_queries = jnp.einsum("hqk,khd->qhd", grad_scores, keys, preferred_element_type=jnp.float32)
    grad_keys = jnp.einsum("hqk,qhd->khd", grad_scores, queries, preferred_element_type=jnp.float32)
    return (grad_queries, grad_keys, grad_values)


def per_slot(attend, items):
    if items[0].shape[0] > 1:
        return lax.map(attend, items)
    return tuple(result[None] for result in attend(tuple(item[0] for item in items)))


def per_device(
    tokens,
    cotangent,
    image_group,
    first_norm_gain_param,
    first_norm_bias,
    w_qkv,
    qv_bias,
    w_out,
    out_bias,
    second_norm_gain_param,
    second_norm_bias,
    w_up,
    up_bias,
    w_down,
    down_bias,
):
    group = lax.axis_index("dp")
    member = lax.axis_index("tensor")
    members = lax.axis_size("tensor")
    local_rows = tokens.shape[0]
    group_rows = local_rows * members
    slot_count = group_rows // SEQ_PAD
    head_cols = w_out.shape[0]
    heads_here = head_cols // HEAD_DIM
    hidden_here = w_up.shape[1]
    tokens_full = gather_rows(tokens)
    qkv_weight, out_weight, up_weight, down_weight = gather_weights(w_qkv, w_out, w_up, w_down)
    pieces = (
        first_norm_gain_param,
        first_norm_bias,
        qv_bias,
        out_bias,
        second_norm_gain_param,
        second_norm_bias,
        up_bias,
        down_bias,
    )
    widths = [piece.shape[0] for piece in pieces]
    packed = lax.all_gather(jnp.concatenate(pieces), ("dp", "tensor"), axis=0)
    ends = [sum(widths[: n + 1]) for n in range(len(widths))]
    (
        first_norm_gain,
        first_norm_shift,
        qv_full,
        out_shift,
        second_norm_gain,
        second_norm_shift,
        up_full,
        down_shift,
    ) = [packed[:, end - width : end].reshape(-1) for width, end in zip(widths, ends)]
    occupied = jnp.sum((image_group == group).astype(jnp.int32))
    positions = jnp.arange(group_rows, dtype=jnp.int32)
    key_valid = ((positions % SEQ_PAD < SEQ) & (positions // SEQ_PAD < occupied)).reshape(
        slot_count, SEQ_PAD
    )
    local_pos = member * local_rows + jnp.arange(local_rows, dtype=jnp.int32)
    row_valid = ((local_pos % SEQ_PAD < SEQ) & (local_pos // SEQ_PAD < occupied)).astype(
        jnp.float32
    )[:, None]
    qv_local = lax.dynamic_slice_in_dim(qv_full, member * 2 * head_cols, 2 * head_cols).reshape(
        2, heads_here, HEAD_DIM
    )
    up_local = lax.dynamic_slice_in_dim(up_full, member * hidden_here, hidden_here)
    layer_inputs = tokens.astype(jnp.float32)
    _, first_standardized, first_inverse_deviation = apply_layer_norm(
        layer_inputs, first_norm_gain, first_norm_shift
    )
    normed_rows, standardized_full, _ = apply_layer_norm(
        tokens_full.astype(jnp.float32), first_norm_gain, first_norm_shift
    )
    normed_full = normed_rows.astype(jnp.bfloat16)
    output_gradient = row_valid * cotangent
    grad_out_full = gather_rows(output_gradient.astype(jnp.bfloat16))
    projected = jnp.dot(normed_full, qkv_weight, preferred_element_type=jnp.float32).reshape(
        group_rows, 3, heads_here, HEAD_DIM
    )
    queries = (projected[:, 0] + qv_local[0]).astype(jnp.bfloat16)
    keys = projected[:, 1].astype(jnp.bfloat16)
    values = (projected[:, 2] + qv_local[1]).astype(jnp.bfloat16)
    shaped = (
        queries.reshape(slot_count, SEQ_PAD, heads_here, HEAD_DIM),
        keys.reshape(slot_count, SEQ_PAD, heads_here, HEAD_DIM),
        values.reshape(slot_count, SEQ_PAD, heads_here, HEAD_DIM),
        key_valid,
    )
    mixed, logsum = per_slot(attend_slot, shaped)
    mixed_rows = mixed.reshape(group_rows, head_cols)
    attn_local = scatter_rows(jnp.dot(mixed_rows, out_weight, preferred_element_type=jnp.float32))
    residual_stream = layer_inputs + attn_local + out_shift
    second_normed_rows, second_standardized, second_inverse_deviation = apply_layer_norm(
        residual_stream, second_norm_gain, second_norm_shift
    )
    normed_two_full = gather_rows(second_normed_rows.astype(jnp.bfloat16))
    hidden = jnp.dot(normed_two_full, up_weight, preferred_element_type=jnp.float32) + up_local
    activated = gelu_value(hidden).astype(jnp.bfloat16)
    mlp_local = scatter_rows(jnp.dot(activated, down_weight, preferred_element_type=jnp.float32))
    output = (row_valid * (residual_stream + mlp_local + down_shift)).astype(jnp.bfloat16)
    down_term = left_product(activated, grad_out_full)
    hidden_gradient = right_product(grad_out_full, down_weight) * gelu_slope(hidden)
    grad_hidden_b = hidden_gradient.astype(jnp.bfloat16)
    up_term = left_product(normed_two_full, grad_hidden_b)
    up_projection_gradient, down_projection_gradient = reduce_grads(up_term, down_term)
    second_normed_gradient = scatter_rows(right_product(grad_hidden_b, up_weight))
    residual_gradient = output_gradient + layer_norm_backward(
        second_normed_gradient, second_standardized, second_inverse_deviation, second_norm_gain
    )
    grad_resid_full = gather_rows(residual_gradient.astype(jnp.bfloat16))
    out_term = left_product(mixed_rows, grad_resid_full)
    grad_mixed = right_product(grad_resid_full, out_weight).astype(jnp.bfloat16)
    back_items = shaped + (
        logsum,
        mixed,
        grad_mixed.reshape(slot_count, SEQ_PAD, heads_here, HEAD_DIM),
    )
    grad_queries, grad_keys, grad_values = per_slot(attend_back, back_items)
    grad_queries = grad_queries.reshape(group_rows, heads_here, HEAD_DIM)
    grad_keys = grad_keys.reshape(group_rows, heads_here, HEAD_DIM)
    grad_values = grad_values.reshape(group_rows, heads_here, HEAD_DIM)
    grad_projected = (
        jnp.stack([grad_queries, grad_keys, grad_values], axis=1)
        .reshape(group_rows, 3 * head_cols)
        .astype(jnp.bfloat16)
    )
    qkv_term = left_product(normed_full, grad_projected)
    query_key_value_gradient, output_projection_gradient = reduce_grads(qkv_term, out_term)
    first_normed_terms = right_product(grad_projected, qkv_weight)
    first_normed_gradient = scatter_rows(first_normed_terms)
    layer_input_gradient = residual_gradient + layer_norm_backward(
        first_normed_gradient, first_standardized, first_inverse_deviation, first_norm_gain
    )
    qv_piece = jnp.concatenate(
        [
            jnp.sum(grad_queries, axis=0).reshape(head_cols),
            jnp.sum(grad_values, axis=0).reshape(head_cols),
        ]
    )
    qv_term = lax.dynamic_update_slice_in_dim(
        jnp.zeros((2 * D,), jnp.float32), qv_piece, member * 2 * head_cols, 0
    )
    up_bias_term = lax.dynamic_update_slice_in_dim(
        jnp.zeros((FF,), jnp.float32), jnp.sum(hidden_gradient, axis=0), member * hidden_here, 0
    )
    vector_terms = (
        jnp.sum(first_normed_terms * standardized_full, axis=0),
        jnp.sum(first_normed_terms, axis=0),
        qv_term,
        jnp.sum(residual_gradient, axis=0),
        jnp.sum(second_normed_gradient * second_standardized, axis=0),
        jnp.sum(second_normed_gradient, axis=0),
        up_bias_term,
        jnp.sum(output_gradient, axis=0),
    )
    packed_terms = jnp.concatenate(
        [term.reshape(-1, width) for term, width in zip(vector_terms, widths)], axis=1
    )
    packed_grad = lax.psum_scatter(
        packed_terms, ("dp", "tensor"), scatter_dimension=0, tiled=False
    )
    (
        gain_one_grad,
        shift_one_grad,
        query_value_bias_gradient,
        out_shift_grad,
        gain_two_grad,
        shift_two_grad,
        up_shift_grad,
        down_shift_grad,
    ) = [packed_grad[end - width : end] for width, end in zip(widths, ends)]
    return (
        output,
        layer_input_gradient,
        gain_one_grad,
        shift_one_grad,
        query_key_value_gradient,
        query_value_bias_gradient,
        output_projection_gradient,
        out_shift_grad,
        gain_two_grad,
        shift_two_grad,
        up_projection_gradient,
        up_shift_grad,
        down_projection_gradient,
        down_shift_grad,
    )


def solution(mesh):
    placed = (
        P(("dp", "tensor"), None),
        P(("dp", "tensor"), None),
        P(),
        P(("dp", "tensor")),
        P(("dp", "tensor")),
        P("dp", "tensor"),
        P(("dp", "tensor")),
        P("tensor", "dp"),
        P(("dp", "tensor")),
        P(("dp", "tensor")),
        P(("dp", "tensor")),
        P("dp", "tensor"),
        P(("dp", "tensor")),
        P("tensor", "dp"),
        P(("dp", "tensor")),
    )
    return jax.shard_map(
        per_device,
        mesh=mesh,
        in_specs=placed,
        out_specs=(
            P(("dp", "tensor"), None),
            P(("dp", "tensor"), None),
            P(("dp", "tensor")),
            P(("dp", "tensor")),
            P("dp", "tensor"),
            P(("dp", "tensor")),
            P("tensor", "dp"),
            P(("dp", "tensor")),
            P(("dp", "tensor")),
            P(("dp", "tensor")),
            P("dp", "tensor"),
            P(("dp", "tensor")),
            P("tensor", "dp"),
            P(("dp", "tensor")),
        ),
        check_vma=False,
    )
```

```python
import functools

import jax
import jax.numpy as jnp
from jax import lax
from jax.experimental import pallas as pl
from jax.experimental.pallas import tpu as pltpu
from jax.sharding import PartitionSpec as P

D = 1024
HEAD_DIM = 64
FF = 4096
SEQ = 577
SEQ_PAD = 640


EPS = 1e-06
NEG_LARGE = -1e30
ROOT_HALF = 0.7071067811865476
INV_ROOT_TAU = 0.3989422804014327


def apply_layer_norm(values, norm_gain_vector, norm_shift_vector):
    average = jnp.mean(values, axis=1, keepdims=True)
    mean_removed = values - average
    variance = jnp.mean(mean_removed * mean_removed, axis=1, keepdims=True)
    inverse_deviation = lax.rsqrt(variance + EPS)
    standardized_rows = mean_removed * inverse_deviation
    return (
        standardized_rows * norm_gain_vector + norm_shift_vector,
        standardized_rows,
        inverse_deviation,
    )


def layer_norm_backward(incoming_gradient, standardized_rows, inverse_deviation, norm_gain_vector):
    gain_scaled_gradient = incoming_gradient * norm_gain_vector
    return inverse_deviation * (
        gain_scaled_gradient
        - jnp.mean(gain_scaled_gradient, axis=1, keepdims=True)
        - standardized_rows
        * jnp.mean(gain_scaled_gradient * standardized_rows, axis=1, keepdims=True)
    )


def gelu_value(hidden):
    return 0.5 * hidden * (1.0 + jax.scipy.special.erf(hidden * ROOT_HALF))


def gelu_slope(hidden):
    return 0.5 * (
        1.0 + jax.scipy.special.erf(hidden * ROOT_HALF)
    ) + hidden * INV_ROOT_TAU * jnp.exp(-0.5 * hidden * hidden)


def left_product(first, second):
    return lax.dot_general(
        first, second, (((0,), (0,)), ((), ())), preferred_element_type=jnp.float32
    )


def right_product(first, second):
    return lax.dot_general(
        first, second, (((1,), (1,)), ((), ())), preferred_element_type=jnp.float32
    )


def gather_rows(values):
    return lax.all_gather(values, "tensor", axis=0, tiled=True)


def scatter_rows(values):
    return lax.psum_scatter(
        values.astype(jnp.bfloat16), "tensor", scatter_dimension=0, tiled=True
    ).astype(jnp.float32)


MESH_ID = pl.DeviceIdType.MESH
LANES = 128
VEC_ROWS = 16


def dp_peers():
    me = lax.axis_index("dp")
    core, along_x, along_y = me % 2, (me // 2) % 2, me // 4
    index = []
    for flip in range(8):
        flip_core, flip_x, flip_y = flip % 2, (flip // 2) % 2, flip // 4
        new_core = 1 - core if flip_core else core
        new_x = 1 - along_x if flip_x else along_x
        new_y = 1 - along_y if flip_y else along_y
        index.append((new_y * 2 + new_x) * 2 + new_core)
    return index


def enter(tensor_size):
    peer = dp_peers()
    barrier = pltpu.get_barrier_semaphore()
    for flip in (1, 2, 4):
        pl.semaphore_signal(
            barrier, inc=1, device_id={"dp": peer[flip]}, device_id_type=MESH_ID
        )
    z_me = lax.axis_index("tensor")
    for hop in range(1, tensor_size):
        pl.semaphore_signal(
            barrier,
            inc=1,
            device_id={"tensor": lax.rem(z_me + hop, tensor_size)},
            device_id_type=MESH_ID,
        )
    pl.semaphore_wait(barrier, 2 + tensor_size)
    return peer, z_me


def part(ref, owner, axis, half=None):
    rows, columns = ref.shape
    if axis == 0:
        size = rows // 8
        start, count = owner * size, size
        if half is not None:
            start, count = start + half * (size // 2), size // 2
        return ref.at[pl.ds(pl.multiple_of(start, count), count), :]
    start, count = 0, rows
    if half is not None:
        start, count = half * (rows // 2), rows // 2
    return ref.at[
        pl.ds(start, count), pl.ds(pl.multiple_of(owner * LANES, LANES), LANES)
    ]


def send(source, target, send_sem, recv_sem, device):
    copy = pltpu.make_async_remote_copy(
        src_ref=source,
        dst_ref=target,
        send_sem=send_sem,
        recv_sem=recv_sem,
        device_id=device,
        device_id_type=MESH_ID,
    )
    copy.start()
    return copy


def gather_kernel(axes, tensor_size, *refs):
    count = len(axes)
    shards, fulls = refs[:count], refs[count : 2 * count]
    vec_all = refs[2 * count]
    send_sems, recv_sems, local_sems, z_send, z_recv = refs[2 * count + 1 :]
    peer, z_me = enter(tensor_size)
    slots = {1: 0, 2: 1, 3: 2, 4: 3, 5: 4, 6: 5, 7: 7}
    sent = []
    locals_ = []

    def give(w, held, half, to, source=None):
        target = part(fulls[w], peer[held], axes[w], half)
        slot = slots[held ^ to] + (half or 0)
        sent.append(
            send(
                target if source is None else source,
                target,
                send_sems.at[w, slots[held ^ to] + (half or 0)],
                recv_sems.at[w, slot],
                {"dp": peer[to]},
            )
        )

    def take(w, held, half):
        block = part(fulls[w], peer[held], axes[w], half)
        pltpu.make_async_copy(block, block, recv_sems.at[w, slots[held] + (half or 0)]).wait()

    for w in range(count):
        own = pltpu.make_async_copy(
            shards[w], part(fulls[w], peer[0], axes[w]), local_sems.at[w]
        )
        own.start()
        locals_.append(own)
        for to in (2, 4, 1):
            give(w, 0, None, to, shards[w])
    for w in range(count):
        take(w, 2, None)
        give(w, 2, 0, 4)
        give(w, 2, None, 1)
        take(w, 4, None)
        give(w, 4, 1, 2)
        give(w, 4, None, 1)
    for w in range(count):
        for half in (0, 1):
            take(w, 6, half)
            give(w, 6, half, 1)
    for own in locals_:
        own.wait()
    order = [count - 1] + list(range(count - 1))
    for w in order:
        for held in (1, 3, 5):
            take(w, held, None)
        for half in (0, 1):
            take(w, 7, half)
        if w == count - 1:
            rows = fulls[w].shape[0]
            place = vec_all.at[pl.ds(pl.multiple_of(z_me * rows, 8), rows), :]
            own = pltpu.make_async_copy(fulls[w], place, local_sems.at[count])
            own.start()
            for hop in range(1, tensor_size):
                sent.append(
                    send(
                        fulls[w],
                        place,
                        z_send.at[hop - 1],
                        z_recv.at[hop - 1],
                        {"tensor": lax.rem(z_me + hop, tensor_size)},
                    )
                )
    rows = fulls[count - 1].shape[0]
    for hop in range(1, tensor_size):
        other = lax.rem(z_me + tensor_size - hop, tensor_size)
        place = vec_all.at[pl.ds(pl.multiple_of(other * rows, 8), rows), :]
        pltpu.make_async_copy(place, place, z_recv.at[hop - 1]).wait()
    own.wait()
    for copy in sent:
        copy.wait_send()


def gather_all(shards, axes, tensor_size):
    count = len(shards)
    sizes = []
    for shard, axis in zip(shards, axes):
        rows, columns = shard.shape
        shape = (rows * 8, columns) if axis == 0 else (rows, columns * 8)
        sizes.append(jax.ShapeDtypeStruct(shape, shard.dtype))
    vec = sizes[-1]
    outs = sizes + [jax.ShapeDtypeStruct((vec.shape[0] * tensor_size, LANES), vec.dtype)]
    vmem = pl.BlockSpec(memory_space=pltpu.VMEM)
    results = pl.pallas_call(
        functools.partial(gather_kernel, axes, tensor_size),
        out_shape=outs,
        in_specs=[vmem] * count,
        out_specs=[pl.BlockSpec(memory_space=pl.ANY)] * (count - 1) + [vmem, vmem],
        scratch_shapes=[
            pltpu.SemaphoreType.DMA((count, 9)),
            pltpu.SemaphoreType.DMA((count, 9)),
            pltpu.SemaphoreType.DMA((count + 1,)),
            pltpu.SemaphoreType.DMA((tensor_size - 1,)),
            pltpu.SemaphoreType.DMA((tensor_size - 1,)),
        ],
        compiler_params=pltpu.CompilerParams(collective_id=0, has_side_effects=True),
        cost_estimate=pl.CostEstimate(
            flops=20_000_000_000, bytes_accessed=80_000_000, transcendentals=0
        ),
    )(*shards)
    return list(results[: count - 1]) + [results[count]]


def reduce_kernel(axes, tensor_size, with_vec, *refs):
    count = len(axes)
    terms, outs = list(refs[:count]), refs[count : 2 * count]
    scratch = refs[2 * count :]
    from_core, sums, from_x, from_y = (
        scratch[n * count : (n + 1) * count] for n in range(4)
    )
    half_in = scratch[4 * count : 5 * count]
    send_sems, recv_sems = scratch[5 * count : 5 * count + 2]
    peer, z_me = enter(tensor_size if with_vec else 1)
    sent = []

    def give(w, source, target, slot, to):
        sent.append(
            send(source, target, send_sems.at[w, slot], recv_sems.at[w, slot], {"dp": peer[to]})
        )

    def take(w, target, slot):
        pltpu.make_async_copy(target, target, recv_sems.at[w, slot]).wait()

    def first(w):
        for k in (3, 1, 2, 0):
            give(w, part(terms[w], peer[1 ^ (2 * k)], axes[w]), from_core[w].at[k], k, 1)

    if with_vec:
        vec_in, vec_sum, z_send, z_recv = scratch[5 * count + 2 :]
        rows = vec_sum.shape[0]
        for hop in range(1, tensor_size):
            other = lax.rem(z_me + hop, tensor_size)
            sent.append(
                send(
                    terms[-1].at[pl.ds(pl.multiple_of(other * rows, 8), rows), :],
                    vec_in.at[hop - 1],
                    z_send.at[hop - 1],
                    z_recv.at[hop - 1],
                    {"tensor": other},
                )
            )
    plain = count - 1 if with_vec else count
    for w in range(plain):
        first(w)
    if with_vec:
        total = terms[-1][pl.ds(pl.multiple_of(z_me * rows, 8), rows), :]
        for hop in range(1, tensor_size):
            pltpu.make_async_copy(
                vec_in.at[hop - 1], vec_in.at[hop - 1], z_recv.at[hop - 1]
            ).wait()
            total = total + vec_in[hop - 1]
        vec_sum[...] = total
        terms[-1] = vec_sum
        first(count - 1)

    def halves(w):
        length = sums[w].shape[1] // 2
        return length, pl.ds(0, length), pl.ds(length, length)

    for w in range(count):
        length, low, high = halves(w)
        for k in (3, 1, 2, 0):
            take(w, from_core[w].at[k], k)
            mine = part(terms[w], peer[2 * k], axes[w])[...]
            sums[w][k] = (
                mine.astype(jnp.float32) + from_core[w][k].astype(jnp.float32)
            ).astype(sums[w].dtype)
            if k == 3:
                give(w, sums[w].at[3, low], half_in[w].at[0], 4, 2)
                give(w, sums[w].at[3, high], half_in[w].at[1], 5, 4)
            if k == 1:
                give(w, sums[w].at[1, low], from_x[w].at[low], 6, 2)
            if k == 2:
                give(w, sums[w].at[2, high], from_y[w].at[high], 7, 4)
    for w in range(count):
        length, low, high = halves(w)
        take(w, half_in[w].at[0], 4)
        sums[w][2, low] = (
            sums[w][2, low].astype(jnp.float32) + half_in[w][0].astype(jnp.float32)
        ).astype(sums[w].dtype)
        give(w, sums[w].at[2, low], from_y[w].at[low], 8, 4)
        take(w, half_in[w].at[1], 5)
        sums[w][1, high] = (
            sums[w][1, high].astype(jnp.float32) + half_in[w][1].astype(jnp.float32)
        ).astype(sums[w].dtype)
        give(w, sums[w].at[1, high], from_x[w].at[high], 9, 2)
    for w in range(count):
        length, low, high = halves(w)
        take(w, from_x[w].at[low], 6)
        take(w, from_y[w].at[high], 7)
        take(w, from_y[w].at[low], 8)
        take(w, from_x[w].at[high], 9)
        outs[w][...] = (
            sums[w][0].astype(jnp.float32)
            + from_x[w][...].astype(jnp.float32)
            + from_y[w][...].astype(jnp.float32)
        )
    for copy in sent:
        copy.wait_send()


def reduce_all(terms, axes, tensor_size, with_vec, collective_id):
    count = len(terms)
    blocks = []
    for n, (term, axis) in enumerate(zip(terms, axes)):
        rows, columns = term.shape
        if with_vec and n == count - 1:
            rows = rows // tensor_size
        blocks.append((rows // 8, columns) if axis == 0 else (rows, columns // 8))
    kinds = [term.dtype for term in terms]
    pairs = list(zip(blocks, kinds))
    scratch = (
        [pltpu.VMEM((4,) + block, kind) for block, kind in pairs]
        + [pltpu.VMEM((4,) + block, kind) for block, kind in pairs]
        + [pltpu.VMEM(block, kind) for block, kind in pairs]
        + [pltpu.VMEM(block, kind) for block, kind in pairs]
        + [pltpu.VMEM((2, block[0] // 2, block[1]), kind) for block, kind in pairs]
        + [pltpu.SemaphoreType.DMA((count, 10)), pltpu.SemaphoreType.DMA((count, 10))]
    )
    if with_vec:
        rows = terms[-1].shape[0] // tensor_size
        scratch += [
            pltpu.VMEM((tensor_size - 1, rows, LANES), jnp.float32),
            pltpu.VMEM((rows, LANES), jnp.float32),
            pltpu.SemaphoreType.DMA((tensor_size - 1,)),
            pltpu.SemaphoreType.DMA((tensor_size - 1,)),
        ]
    vmem = pl.BlockSpec(memory_space=pltpu.VMEM)
    return pl.pallas_call(
        functools.partial(reduce_kernel, axes, tensor_size, with_vec),
        out_shape=[jax.ShapeDtypeStruct(block, jnp.float32) for block in blocks],
        in_specs=[vmem] * count,
        out_specs=[vmem] * count,
        scratch_shapes=scratch,
        compiler_params=pltpu.CompilerParams(
            collective_id=collective_id, has_side_effects=True
        ),
        cost_estimate=pl.CostEstimate(
            flops=15_000_000_000, bytes_accessed=60_000_000, transcendentals=0
        ),
    )(*terms)


def gather_weights(w_qkv, w_out, w_up, w_down):
    return (
        lax.all_gather(w_qkv, "dp", axis=0, tiled=True),
        lax.all_gather(w_out, "dp", axis=1, tiled=True),
        lax.all_gather(w_up, "dp", axis=0, tiled=True),
        lax.all_gather(w_down, "dp", axis=1, tiled=True),
    )


def reduce_grads(row_split, column_split):
    return (
        lax.psum_scatter(
            row_split.astype(jnp.bfloat16), "dp", scatter_dimension=0, tiled=True
        ).astype(jnp.float32),
        lax.psum_scatter(
            column_split.astype(jnp.bfloat16), "dp", scatter_dimension=1, tiled=True
        ).astype(jnp.float32),
    )


def masked_scores(queries, keys, key_valid):
    scores = jnp.einsum(
        "qhd,khd->hqk", queries, keys, preferred_element_type=jnp.float32
    ) * HEAD_DIM ** (-0.5)
    return jnp.where(key_valid[None, None, :], scores, NEG_LARGE)


def attend_slot(items):
    queries, keys, values, key_valid = items
    scores = masked_scores(queries, keys, key_valid)
    top = jnp.max(scores, axis=2, keepdims=True)
    total = jnp.sum(jnp.exp(scores - top), axis=2, keepdims=True)
    logsum = top + jnp.log(total)
    probs = jnp.exp(scores - logsum).astype(jnp.bfloat16)
    mixed = jnp.einsum("hqk,khd->qhd", probs, values, preferred_element_type=jnp.float32).astype(
        jnp.bfloat16
    )
    return (mixed, logsum[:, :, 0])


def attend_back(items):
    queries, keys, values, key_valid, logsum, mixed, grad_mixed = items
    scores = masked_scores(queries, keys, key_valid)
    probs = jnp.exp(scores - logsum[:, :, None])
    rounded = probs.astype(jnp.bfloat16)
    grad_values = jnp.einsum(
        "hqk,qhd->khd", rounded, grad_mixed, preferred_element_type=jnp.float32
    )
    grad_probs = jnp.einsum("qhd,khd->hqk", grad_mixed, values, preferred_element_type=jnp.float32)
    delta = jnp.sum(grad_mixed.astype(jnp.float32) * mixed.astype(jnp.float32), axis=2).T
    grad_scores = (probs * (grad_probs - delta[:, :, None]) * HEAD_DIM ** (-0.5)).astype(
        jnp.bfloat16
    )
    grad_queries = jnp.einsum("hqk,khd->qhd", grad_scores, keys, preferred_element_type=jnp.float32)
    grad_keys = jnp.einsum("hqk,qhd->khd", grad_scores, queries, preferred_element_type=jnp.float32)
    return (grad_queries, grad_keys, grad_values)


def per_slot(attend, items):
    if items[0].shape[0] > 1:
        return lax.map(attend, items)
    return tuple(result[None] for result in attend(tuple(item[0] for item in items)))


def per_device(
    tokens,
    cotangent,
    image_group,
    first_norm_gain_param,
    first_norm_bias,
    w_qkv,
    qv_bias,
    w_out,
    out_bias,
    second_norm_gain_param,
    second_norm_bias,
    w_up,
    up_bias,
    w_down,
    down_bias,
):
    group = lax.axis_index("dp")
    member = lax.axis_index("tensor")
    members = lax.axis_size("tensor")
    local_rows = tokens.shape[0]
    group_rows = local_rows * members
    slot_count = group_rows // SEQ_PAD
    head_cols = w_out.shape[0]
    heads_here = head_cols // HEAD_DIM
    hidden_here = w_up.shape[1]
    tokens_full = gather_rows(tokens)
    use_kernels = lax.axis_size("dp") == 8 and members > 1
    pieces = (
        first_norm_gain_param,
        first_norm_bias,
        qv_bias,
        out_bias,
        second_norm_gain_param,
        second_norm_bias,
        up_bias,
        down_bias,
    )
    widths = [piece.shape[0] for piece in pieces]
    packed = jnp.concatenate(pieces)
    length = packed.shape[0]
    if use_kernels:
        vec = jnp.zeros((VEC_ROWS * LANES,), jnp.float32).at[:length].set(packed)
        qkv_weight, out_weight, up_weight, down_weight, everyone = gather_all(
            (w_qkv, w_out, w_up, w_down, vec.reshape(VEC_ROWS, LANES)), (0, 1, 0, 1, 0), members
        )
        packed = (
            everyone.reshape(members, 8, VEC_ROWS * LANES)[:, :, :length]
            .transpose(1, 0, 2)
            .reshape(8 * members, length)
        )
    else:
        qkv_weight, out_weight, up_weight, down_weight = gather_weights(
            w_qkv, w_out, w_up, w_down
        )
        packed = lax.all_gather(packed, ("dp", "tensor"), axis=0)
    ends = [sum(widths[: n + 1]) for n in range(len(widths))]
    (
        first_norm_gain,
        first_norm_shift,
        qv_full,
        out_shift,
        second_norm_gain,
        second_norm_shift,
        up_full,
        down_shift,
    ) = [packed[:, end - width : end].reshape(-1) for width, end in zip(widths, ends)]
    occupied = jnp.sum((image_group == group).astype(jnp.int32))
    positions = jnp.arange(group_rows, dtype=jnp.int32)
    key_valid = ((positions % SEQ_PAD < SEQ) & (positions // SEQ_PAD < occupied)).reshape(
        slot_count, SEQ_PAD
    )
    local_pos = member * local_rows + jnp.arange(local_rows, dtype=jnp.int32)
    row_valid = ((local_pos % SEQ_PAD < SEQ) & (local_pos // SEQ_PAD < occupied)).astype(
        jnp.float32
    )[:, None]
    qv_local = lax.dynamic_slice_in_dim(qv_full, member * 2 * head_cols, 2 * head_cols).reshape(
        2, heads_here, HEAD_DIM
    )
    up_local = lax.dynamic_slice_in_dim(up_full, member * hidden_here, hidden_here)
    layer_inputs = tokens.astype(jnp.float32)
    _, first_standardized, first_inverse_deviation = apply_layer_norm(
        layer_inputs, first_norm_gain, first_norm_shift
    )
    normed_rows, standardized_full, _ = apply_layer_norm(
        tokens_full.astype(jnp.float32), first_norm_gain, first_norm_shift
    )
    normed_full = normed_rows.astype(jnp.bfloat16)
    output_gradient = row_valid * cotangent
    grad_out_full = gather_rows(output_gradient.astype(jnp.bfloat16))
    projected = jnp.dot(normed_full, qkv_weight, preferred_element_type=jnp.float32).reshape(
        group_rows, 3, heads_here, HEAD_DIM
    )
    queries = (projected[:, 0] + qv_local[0]).astype(jnp.bfloat16)
    keys = projected[:, 1].astype(jnp.bfloat16)
    values = (projected[:, 2] + qv_local[1]).astype(jnp.bfloat16)
    shaped = (
        queries.reshape(slot_count, SEQ_PAD, heads_here, HEAD_DIM),
        keys.reshape(slot_count, SEQ_PAD, heads_here, HEAD_DIM),
        values.reshape(slot_count, SEQ_PAD, heads_here, HEAD_DIM),
        key_valid,
    )
    mixed, logsum = per_slot(attend_slot, shaped)
    mixed_rows = mixed.reshape(group_rows, head_cols)
    mixed_rows, grad_out_full = lax.optimization_barrier((mixed_rows, grad_out_full))
    attn_local = scatter_rows(jnp.dot(mixed_rows, out_weight, preferred_element_type=jnp.float32))
    residual_stream = layer_inputs + attn_local + out_shift
    second_normed_rows, second_standardized, second_inverse_deviation = apply_layer_norm(
        residual_stream, second_norm_gain, second_norm_shift
    )
    normed_two_full = gather_rows(second_normed_rows.astype(jnp.bfloat16))
    hidden = jnp.dot(normed_two_full, up_weight, preferred_element_type=jnp.float32) + up_local
    activated = gelu_value(hidden).astype(jnp.bfloat16)
    down_term = left_product(activated, grad_out_full)
    hidden_gradient = right_product(grad_out_full, down_weight) * gelu_slope(hidden)
    grad_hidden_b = hidden_gradient.astype(jnp.bfloat16)
    up_term = left_product(normed_two_full, grad_hidden_b)
    if use_kernels:
        up_projection_gradient, down_projection_gradient = reduce_all(
            (up_term.astype(jnp.bfloat16), down_term.astype(jnp.bfloat16)),
            (0, 1),
            members,
            False,
            1,
        )
    else:
        up_projection_gradient, down_projection_gradient = reduce_grads(up_term, down_term)
    second_normed_gradient = scatter_rows(right_product(grad_hidden_b, up_weight))
    residual_gradient = output_gradient + layer_norm_backward(
        second_normed_gradient, second_standardized, second_inverse_deviation, second_norm_gain
    )
    grad_resid_full = gather_rows(residual_gradient.astype(jnp.bfloat16))
    mlp_terms = jnp.dot(activated, down_weight, preferred_element_type=jnp.float32)
    mlp_terms, grad_resid_full, up_projection_gradient = lax.optimization_barrier(
        (mlp_terms.astype(jnp.bfloat16), grad_resid_full, up_projection_gradient)
    )
    mlp_local = scatter_rows(mlp_terms)
    output = (row_valid * (residual_stream + mlp_local + down_shift)).astype(jnp.bfloat16)
    out_term = left_product(mixed_rows, grad_resid_full)
    grad_mixed = right_product(grad_resid_full, out_weight).astype(jnp.bfloat16)
    back_items = shaped + (
        logsum,
        mixed,
        grad_mixed.reshape(slot_count, SEQ_PAD, heads_here, HEAD_DIM),
    )
    grad_queries, grad_keys, grad_values = per_slot(attend_back, back_items)
    grad_queries = grad_queries.reshape(group_rows, heads_here, HEAD_DIM)
    grad_keys = grad_keys.reshape(group_rows, heads_here, HEAD_DIM)
    grad_values = grad_values.reshape(group_rows, heads_here, HEAD_DIM)
    grad_projected = (
        jnp.stack([grad_queries, grad_keys, grad_values], axis=1)
        .reshape(group_rows, 3 * head_cols)
        .astype(jnp.bfloat16)
    )
    qkv_term = left_product(normed_full, grad_projected)
    first_normed_terms = right_product(grad_projected, qkv_weight)
    first_normed_gradient = scatter_rows(first_normed_terms)
    layer_input_gradient = residual_gradient + layer_norm_backward(
        first_normed_gradient, first_standardized, first_inverse_deviation, first_norm_gain
    )
    qv_piece = jnp.concatenate(
        [
            jnp.sum(grad_queries, axis=0).reshape(head_cols),
            jnp.sum(grad_values, axis=0).reshape(head_cols),
        ]
    )
    qv_bias_term = lax.dynamic_update_slice_in_dim(
        jnp.zeros((2 * D,), jnp.float32), qv_piece, member * 2 * head_cols, 0
    )
    up_bias_term = lax.dynamic_update_slice_in_dim(
        jnp.zeros((FF,), jnp.float32), jnp.sum(hidden_gradient, axis=0), member * hidden_here, 0
    )
    vector_terms = (
        jnp.sum(first_normed_terms * standardized_full, axis=0),
        jnp.sum(first_normed_terms, axis=0),
        qv_bias_term,
        jnp.sum(residual_gradient, axis=0),
        jnp.sum(second_normed_gradient * second_standardized, axis=0),
        jnp.sum(second_normed_gradient, axis=0),
        up_bias_term,
        jnp.sum(output_gradient, axis=0),
    )
    packed_terms = jnp.concatenate(
        [term.reshape(-1, width) for term, width in zip(vector_terms, widths)], axis=1
    )
    if use_kernels:
        spread = jnp.pad(packed_terms, ((0, 0), (0, VEC_ROWS * LANES - length)))
        spread = spread.reshape(8, members, VEC_ROWS, LANES).transpose(1, 0, 2, 3)
        query_key_value_gradient, output_projection_gradient, packed_grad = reduce_all(
            (
                qkv_term.astype(jnp.bfloat16),
                out_term.astype(jnp.bfloat16),
                spread.reshape(members * 8 * VEC_ROWS, LANES),
            ),
            (0, 1, 0),
            members,
            True,
            2,
        )
        packed_grad = packed_grad.reshape(-1)[:length]
    else:
        query_key_value_gradient, output_projection_gradient = reduce_grads(qkv_term, out_term)
        packed_grad = lax.psum_scatter(
            packed_terms, ("dp", "tensor"), scatter_dimension=0, tiled=False
        )
    (
        gain_one_grad,
        shift_one_grad,
        query_value_bias_gradient,
        out_shift_grad,
        gain_two_grad,
        shift_two_grad,
        up_shift_grad,
        down_shift_grad,
    ) = [packed_grad[end - width : end] for width, end in zip(widths, ends)]
    return (
        output,
        layer_input_gradient,
        gain_one_grad,
        shift_one_grad,
        query_key_value_gradient,
        query_value_bias_gradient,
        output_projection_gradient,
        out_shift_grad,
        gain_two_grad,
        shift_two_grad,
        up_projection_gradient,
        up_shift_grad,
        down_projection_gradient,
        down_shift_grad,
    )


def solution(mesh):
    placed = (
        P(("dp", "tensor"), None),
        P(("dp", "tensor"), None),
        P(),
        P(("dp", "tensor")),
        P(("dp", "tensor")),
        P("dp", "tensor"),
        P(("dp", "tensor")),
        P("tensor", "dp"),
        P(("dp", "tensor")),
        P(("dp", "tensor")),
        P(("dp", "tensor")),
        P("dp", "tensor"),
        P(("dp", "tensor")),
        P("tensor", "dp"),
        P(("dp", "tensor")),
    )
    return jax.shard_map(
        per_device,
        mesh=mesh,
        in_specs=placed,
        out_specs=(
            P(("dp", "tensor"), None),
            P(("dp", "tensor"), None),
            P(("dp", "tensor")),
            P(("dp", "tensor")),
            P("dp", "tensor"),
            P(("dp", "tensor")),
            P("tensor", "dp"),
            P(("dp", "tensor")),
            P(("dp", "tensor")),
            P(("dp", "tensor")),
            P("dp", "tensor"),
            P(("dp", "tensor")),
            P("tensor", "dp"),
            P(("dp", "tensor")),
        ),
        check_vma=False,
    )
```
